32 devices in a mesh: grp: 2 (over y), ta: 4 (over z), gx: 4 (over x, core).
Axes of the slice: x: 2, y: 2, z: 4, core: 2. Of those that a mesh axis runs over, the one named last changes fastest.
Arguments:
- vectors: bfloat16 [8, 2, 3, 8192, 128], P(('grp', 'ta'), None, None, 'gx'), parts along dimension 0, may hold values from -6 to 6
- peramb: bfloat16 [8, 16, 2, 128, 128], P(('grp', 'ta')), parts along dimension 0, may hold values from -0.5 to 0.5
- momenta: int32 [8, 3], P('grp'), parts along dimension 0, may hold values from -2 to 2, as said below
- sink_mom: int32 [32], P('grp'), parts along dimension 0, may hold values from 0 to 3
- spin_pick: int32 [32], P('grp'), parts along dimension 0, may hold values from 0 to 15
- src_time: int32 [2], P('grp'), parts along dimension 0, may hold values from 0 to 65535
Outputs:
- corr: float32 [8, 16, 2, 128, 128], P(('grp', 'ta'), 'gx'), parts along dimension 0
The draws below stay inside these ranges and needn't reach their ends.
There are 2 independent parts, one for each index of `grp`. The reference program is written for one: setup_inputs(seed, part) draws one part's arguments, and reference() takes and returns one part's arrays. A program takes and returns all parts, laid end to end along the dimension named above; each array names one. Nothing has to cross between parts.
Inputs may be any that keep to these rules, and one draw needn't show every extreme that they name: `momenta`: every component of every momentum is nonzero.
All inputs are finite; a program needn't handle non-finite values.
Results may differ from the reference program's by a relative error of at most 0.0038.
Values sent between devices are 32-bit elements; how exact they have to be, the bound alone decides.
A program may use at most 64 MiB of HBM per device.

```python
import math
import jax
import jax.numpy as jnp
from jax import lax

RANK = 128
LY = 32
LZ = 32
NMOM = 4
SPIN_BLOCKS = 16
SPINS = 16
NSITES = 8192
NT = 4


def draw_momenta(key, part):
    magnitude = jax.random.randint(jax.random.fold_in(key, 11), (NMOM, 3), 1, 3)
    signed = jax.random.randint(jax.random.fold_in(key, 12), (NMOM, 3), 0, 2) * 2 - 1
    return (magnitude * signed).astype(jnp.int32)


def plant(array, rng, smallest, top_value):
    longest = array.shape.index(max(array.shape))
    spots = []
    for shift in (0, 1):
        where = [jax.random.randint(jax.random.fold_in(rng, axis), (), 0, length) for axis, length in enumerate(array.shape)]
        where[longest] = (where[longest] + shift) % array.shape[longest]
        spots.append(tuple(where))
    return array.at[spots[0]].set(smallest).at[spots[1]].set(top_value)


def level_of(key, shape, split, smallest, top_value):
    def one(position, parts):
        heights = jax.random.uniform(jax.random.fold_in(jax.random.fold_in(key, 6), position), (parts,), jnp.float32, smallest / len(split), top_value / len(split))
        return jnp.repeat(jnp.exp(heights), shape[position] // parts).reshape((-1,) + (1,) * (len(shape) - position - 1))

    loudness = one(*split[0])
    for cut in split[1:]:
        loudness = loudness * one(*cut)
    return loudness


def bell_draw(stream_key, dims, deviation, bound, shards=(), kind=jnp.bfloat16):
    entries = deviation * jax.random.normal(stream_key, dims, jnp.float32)
    if shards:
        entries = entries * level_of(stream_key, dims, shards, -0.22, 0.18)
    return jnp.clip(entries, -bound, bound).astype(kind)


def setup_inputs(seed: int = 0, part: int = 0) -> dict:
    key_of = jax.random.split(jax.random.key(seed), 7)
    own_keys = jax.random.split(jax.random.fold_in(key_of[6], part), 7)
    vectors = bell_draw(own_keys[0], (NT, 2, 3, NSITES, RANK), 1.0, 6.0, ((0, 4), (3, 4)))
    peramb = bell_draw(own_keys[1], (NT, SPIN_BLOCKS, 2, RANK, RANK), RANK ** -0.5, 0.5, ((0, 4),))
    momenta = draw_momenta(jax.random.fold_in(jax.random.fold_in(key_of[6], part), 71), part)
    sink_mom = plant(jax.random.randint(own_keys[3], (SPINS,), 0, NMOM), jax.random.fold_in(own_keys[3], 1), 0, NMOM - 1).astype(jnp.int32)
    spin_pick = plant(jax.random.randint(own_keys[4], (SPINS,), 0, SPIN_BLOCKS), jax.random.fold_in(own_keys[4], 1), 0, SPIN_BLOCKS - 1).astype(jnp.int32)
    src_time = jax.random.randint(own_keys[5], (1,), 0, 65536).astype(jnp.int32)
    return {"vectors": vectors, "peramb": peramb, "momenta": momenta, "sink_mom": sink_mom, "spin_pick": spin_pick, "src_time": src_time}


def phase_angle(momentum, first_x, count, extent_x):
    site_ids = jnp.arange(count, dtype=jnp.int32)
    coord_x = (first_x + site_ids // (LY * LZ)).astype(jnp.int32)
    coord_y = site_ids // LZ % LY
    coord_z = site_ids % LZ
    part_x = jnp.mod(momentum[0] * coord_x, extent_x).astype(jnp.float32) / extent_x
    part_y = jnp.mod(momentum[1] * coord_y, LY).astype(jnp.float32) / LY
    part_z = jnp.mod(momentum[2] * coord_z, LZ).astype(jnp.float32) / LZ
    return 2.0 * math.pi * (part_x + part_y + part_z)

def elemental(vec_re, vec_im, angle, scale):
    cos_part = jnp.cos(angle)[None, :, None]
    sin_part = jnp.sin(angle)[None, :, None]
    real_f = vec_re.astype(jnp.float32)
    imag_f = vec_im.astype(jnp.float32)
    phased_re = real_f * cos_part + imag_f * sin_part
    phased_im = imag_f * cos_part - real_f * sin_part
    upper = jnp.concatenate([phased_re, phased_im], axis=-1)
    lower = jnp.concatenate([phased_im, -phased_re], axis=-1)
    phased = jnp.concatenate([upper, lower], axis=0).astype(jnp.bfloat16)
    total_rows = phased.shape[0] * phased.shape[1]
    phased = phased.reshape(total_rows, -1)
    stacked = jnp.concatenate([vec_re, vec_im], axis=0).reshape(total_rows, -1)
    product = lax.dot_general(stacked, phased, (((0,), (0,)), ((), ())), preferred_element_type=jnp.float32) * scale
    width = vec_re.shape[-1]
    return jnp.stack([product[:, :width], product[:, width:]])

def matmul_high(left, right):
    return jnp.matmul(left, right, precision=lax.Precision.HIGHEST)

def complex_mul(left, right):
    real_part = matmul_high(left[..., 0, :, :], right[..., 0, :, :]) - matmul_high(left[..., 1, :, :], right[..., 1, :, :])
    imag_part = matmul_high(left[..., 0, :, :], right[..., 1, :, :]) + matmul_high(left[..., 1, :, :], right[..., 0, :, :])
    return jnp.stack([real_part, imag_part], axis=-3)

def reference(vectors, peramb, momenta, sink_mom, spin_pick, src_time):
    sites = vectors.shape[3]
    extent_x = sites // (LY * LZ)
    scale = 1.0 / math.sqrt(vectors.shape[2] * sites)
    angles = jnp.stack([phase_angle(momenta[m], 0, sites, extent_x) for m in range(NMOM)])

    def one_slice(vec_slice):
        return jnp.stack([elemental(vec_slice[0], vec_slice[1], angles[m], scale) for m in range(NMOM)])
    elems = lax.map(one_slice, vectors)
    source = elems[jnp.mod(src_time[0], NT).astype(jnp.int32), 0]
    chosen = peramb[:, spin_pick].astype(jnp.float32)
    half_prod = complex_mul(chosen, source)
    sink = elems[:, sink_mom]
    return complex_mul(sink, half_prod) / math.sqrt(RANK)
```

```python
import functools
import math

import jax
import jax.numpy as jnp
from jax import lax
from jax.experimental import pallas as pl
from jax.experimental.pallas import tpu as pltpu
from jax.sharding import PartitionSpec as P

LY = 32
LZ = 32
MESH = pl.DeviceIdType.MESH
F32 = jnp.float32
BF16 = jnp.bfloat16


def split(value):
    high = value.astype(BF16)
    low = (value - high.astype(F32)).astype(BF16)
    return high, low


def mxu(left, right):
    return lax.dot_general(left, right, (((1,), (0,)), ((), ())), preferred_element_type=F32)


def complex_block(re, im):
    return jnp.concatenate(
        [jnp.concatenate([re, im], axis=1), jnp.concatenate([-im, re], axis=1)], axis=0
    )


def kernel(
    n, nt, chunk, piece,
    mom_hbm, sink_hbm, pick_hbm, time_hbm, vec_hbm, per_hbm,
    out_ref,
    mom_ref, sink_ref, pick_ref, time_ref,
    ab, trans, trig, acc, per, part, rx1, s1, rx2, full, tabuf, src, half,
    int_sem, vec_sem, per_sem, ta_s, ta_r, sl_s, sl_r,
    x1_s, x1_r, x2_s, x2_r, x3_s, x3_r,
):
    nmom = part.shape[0]
    rank = part.shape[-1]
    colours, sites = ab.shape[0], ab.shape[1]
    blocks = out_ref.shape[1]
    rows = rank // n
    hrows = rank // 2
    g = lax.axis_index("gx")
    t = lax.axis_index("ta")
    core = lax.rem(g, 2)
    partner = g + 1 - 2 * core
    chips = n // 2

    def ahead(d):
        return lax.rem(g + d, n)

    def remote(src_ref, dst_ref, ss, rs, **where):
        return pltpu.make_async_remote_copy(
            src_ref=src_ref, dst_ref=dst_ref, send_sem=ss, recv_sem=rs,
            device_id=where, device_id_type=MESH,
        )

    integers = [
        pltpu.make_async_copy(where, to, int_sem.at[i])
        for i, (where, to) in enumerate(
            [(mom_hbm, mom_ref), (sink_hbm, sink_ref), (pick_hbm, pick_ref), (time_hbm, time_ref)]
        )
    ]
    for load in integers:
        load.start()
    barrier = pltpu.get_barrier_semaphore()
    for d in range(1, n):
        pl.semaphore_signal(barrier, inc=1, device_id={"gx": ahead(d)}, device_id_type=MESH)
    for d in range(1, nt):
        pl.semaphore_signal(
            barrier, inc=1, device_id={"ta": lax.rem(t + d, nt)}, device_id_type=MESH
        )

    loads = []
    for col in range(colours):
        for ri in range(2):
            load = pltpu.make_async_copy(
                vec_hbm.at[0, ri, col],
                ab.at[col, :, pl.ds(ri * rank, rank)],
                vec_sem.at[col, ri],
            )
            load.start()
            loads.append(load)
    per_load = pltpu.make_async_copy(per_hbm.at[0], per, per_sem)
    per_load.start()

    for load in integers:
        load.wait()

    slab_x = sites // (LY * LZ)
    shape = (8, sites)
    row = lax.broadcasted_iota(jnp.int32, shape, 0)
    site = lax.broadcasted_iota(jnp.int32, shape, 1)

    def component(axis):
        value = jnp.zeros(shape, F32)
        for m in range(nmom):
            value = jnp.where(row == m, mom_ref[m, axis].astype(F32), value)
        return value

    x = (g * slab_x + lax.shift_right_logical(site, int(math.log2(LY * LZ)))).astype(F32)
    y = (lax.shift_right_logical(site, int(math.log2(LZ))) & (LY - 1)).astype(F32)
    z = (site & (LZ - 1)).astype(F32)
    turns = (
        component(0) * x * (1.0 / (slab_x * n))
        + component(1) * y * (1.0 / LY)
        + component(2) * z * (1.0 / LZ)
    )
    turns = turns - jnp.floor(turns + 0.5)
    angle = (2.0 * math.pi) * turns
    trig[0] = jnp.cos(angle)
    trig[1] = jnp.sin(angle)

    scale = 1.0 / math.sqrt(colours * sites * n)

    def accumulate(p, col):
        @pl.loop(0, sites // chunk)
        def _(i):
            at = pl.ds(pl.multiple_of(i * chunk, chunk), chunk)
            a = trans[col, 0, :, at]
            b = trans[col, 1, :, at]
            c = trig[0, p : p + 1, at]
            s = trig[1, p : p + 1, at]
            phased = jnp.concatenate(
                [(a * c + b * s).astype(BF16), (b * c - a * s).astype(BF16)], axis=0
            )
            acc[...] += mxu(phased, ab[col, at, :])

    def finish(p):
        part[p, 0] = (acc[:rank, :rank] + acc[rank:, rank:]).T * scale
        part[p, 1] = (acc[rank:, :rank] - acc[:rank, rank:]).T * scale

    def band(at, size):
        return pl.ds(pl.multiple_of(at * size, size), size)

    mine = pl.ds(pl.multiple_of(core * hrows + lax.div(g, 2) * rows, rows), rows)
    sends = []

    def ta_copy(d):
        return remote(
            tabuf.at[t], tabuf.at[t], ta_s.at[d - 1], ta_r.at[d - 1], ta=lax.rem(t + d, nt)
        )

    def sl_copy(d):
        return remote(
            src.at[:, mine], src.at[:, mine], sl_s.at[d - 1], sl_r.at[d - 1], gx=ahead(d)
        )

    def x1_copy(p):
        return remote(
            part.at[p, :, band(1 - core, hrows)], rx1.at[p], x1_s.at[p], x1_r.at[p],
            gx=partner,
        )

    def x2_copy(p, d):
        return remote(
            s1.at[p], rx2.at[p, d - 1], x2_s.at[p, d - 1], x2_r.at[p, d - 1],
            gx=ahead(2 * d),
        )

    def x3_copy(p):
        keep = full.at[p, :, band(core, hrows)]
        return remote(keep, keep, x3_s.at[p], x3_r.at[p], gx=partner)

    def go(copy):
        copy.start()
        sends.append(copy)

    def p0_select():
        for d in range(1, nt):
            ta_copy(d).wait_recv()
        root = lax.rem(time_ref[0], nt)
        src[:, mine] = tabuf[root]
        for d in range(1, n):
            go(sl_copy(d))

    def step2(p):
        x1_copy(p).wait_recv()
        s1[p] = part[p, :, band(core, hrows)] + rx1[p]
        for d in range(1, chips):
            go(x2_copy(p, d))

    def step3(p):
        total = s1[p]
        for d in range(1, chips):
            x2_copy(p, d).wait_recv()
            total = total + rx2[p, d - 1]
        full[p, :, band(core, hrows)] = total
        if p == 0:
            tabuf[t] = full[0, :, mine]
            for d in range(1, nt):
                go(ta_copy(d))
        go(x3_copy(p))

    acc[...] = jnp.zeros_like(acc)
    for col in range(colours):
        loads[2 * col].wait()
        loads[2 * col + 1].wait()

        @pl.loop(0, sites // piece)
        def _(i):
            at = pl.ds(pl.multiple_of(i * piece, piece), piece)
            for ri in range(2):
                trans[col, ri, :, at] = ab[col, at, ri * rank : (ri + 1) * rank].astype(F32).T

        accumulate(0, col)
    finish(0)
    pl.semaphore_wait(barrier, n + nt - 2)
    go(x1_copy(0))
    for p in range(1, nmom):
        acc[...] = jnp.zeros_like(acc)
        for col in range(colours):
            accumulate(p, col)
        finish(p)
        go(x1_copy(p))
        if p == 1:
            step2(0)
        if p == 3:
            step2(1)
    if nmom == 1:
        step2(0)
    step3(0)
    for p in range(2 if nmom > 3 else 1, nmom):
        step2(p)
    for p in range(1, nmom):
        if p == nmom - 1:
            p0_select()
        step3(p)
    if nmom == 1:
        p0_select()

    per_load.wait()
    for p in range(nmom):
        x3_copy(p).wait_recv()
    for j in range(blocks):
        sink = sink_ref[g * blocks + j]
        pick = pick_ref[g * blocks + j]
        e_high, e_low = split(jnp.concatenate([full[sink, 0], full[sink, 1]], axis=1))
        spin = complex_block(per[pick, 0], per[pick, 1])
        half[j * rank : (j + 1) * rank] = mxu(e_high, spin) + mxu(e_low, spin)
    h_high, h_low = split(half[...] * (1.0 / math.sqrt(rank)))
    for d in range(1, n):
        sl_copy(d).wait_recv()
    s_high, s_low = split(complex_block(src[0], src[1]))
    for j in range(blocks):
        at = slice(j * rank, (j + 1) * rank)
        corr = mxu(h_high[at], s_high) + mxu(h_high[at], s_low) + mxu(h_low[at], s_high)
        out_ref[0, j, 0] = corr[:, :rank]
        out_ref[0, j, 1] = corr[:, rank:]
    for copy in sends:
        copy.wait_send()


def in_hbm(array):
    return pltpu.with_memory_space_constraint(array, pltpu.HBM)


def body(vectors, peramb, momenta, sink_mom, spin_pick, src_time):
    n = lax.axis_size("gx")
    nt = lax.axis_size("ta")
    colours, sites, rank = vectors.shape[2:]
    nmom = momenta.shape[0]
    spins = sink_mom.shape[0]
    blocks = spins // n
    rows = rank // n
    chips = n // 2
    chunk = min(2048, sites)
    dma = pltpu.SemaphoreType.DMA
    hbm = pl.BlockSpec(memory_space=pl.ANY)
    return pl.pallas_call(
        functools.partial(kernel, n, nt, chunk, min(2048, sites)),
        out_shape=pltpu.VMEM((1, blocks, 2, rank, rank), F32),
        in_specs=[hbm] * 6,
        out_specs=pl.BlockSpec(memory_space=pltpu.VMEM),
        scratch_shapes=[
            pltpu.SMEM(momenta.shape, jnp.int32),
            pltpu.SMEM(sink_mom.shape, jnp.int32),
            pltpu.SMEM(spin_pick.shape, jnp.int32),
            pltpu.SMEM(src_time.shape, jnp.int32),
            pltpu.VMEM((colours, sites, 2 * rank), BF16),
            pltpu.VMEM((colours, 2, rank, sites), F32),
            pltpu.VMEM((2, 8, sites), F32),
            pltpu.VMEM((2 * rank, 2 * rank), F32),
            pltpu.VMEM(peramb.shape[1:], BF16),
            pltpu.VMEM((nmom, 2, rank, rank), F32),
            pltpu.VMEM((nmom, 2, rank // 2, rank), F32),
            pltpu.VMEM((nmom, 2, rank // 2, rank), F32),
            pltpu.VMEM((nmom, max(chips - 1, 1), 2, rank // 2, rank), F32),
            pltpu.VMEM((nmom, 2, rank, rank), F32),
            pltpu.VMEM((nt, 2, rows, rank), F32),
            pltpu.VMEM((2, rank, rank), F32),
            pltpu.VMEM((blocks * rank, 2 * rank), F32),
            dma((4,)),
            dma((colours, 2)),
            dma,
            dma((max(nt - 1, 1),)), dma((max(nt - 1, 1),)),
            dma((n - 1,)), dma((n - 1,)),
            dma((nmom,)), dma((nmom,)),
            dma((nmom, max(chips - 1, 1))), dma((nmom, max(chips - 1, 1))),
            dma((nmom,)), dma((nmom,)),
        ],
        compiler_params=pltpu.CompilerParams(
            collective_id=0, has_side_effects=True, vmem_limit_bytes=50*2**20
        ),
    )(
        in_hbm(momenta), in_hbm(sink_mom), in_hbm(spin_pick), src_time,
        in_hbm(vectors), in_hbm(peramb),
    )


def solution(mesh):
    placed = (
        P(("grp", "ta"), None, None, "gx", None),
        P(("grp", "ta"), None, None, None, None),
        P("grp", None),
        P("grp"),
        P("grp"),
        P("grp"),
    )
    return jax.shard_map(
        body,
        mesh=mesh,
        in_specs=placed,
        out_specs=P(("grp", "ta"), "gx", None, None, None),
        check_vma=False,
    )
```

```python
import functools
import math

import jax
import jax.numpy as jnp
from jax import lax
from jax.experimental import pallas as pl
from jax.experimental.pallas import tpu as pltpu
from jax.sharding import PartitionSpec as P

LY = 32
LZ = 32
MESH = pl.DeviceIdType.MESH
F32 = jnp.float32
BF16 = jnp.bfloat16


def split(value):
    high = value.astype(BF16)
    low = (value - high.astype(F32)).astype(BF16)
    return high, low


def mxu(left, right):
    return lax.dot_general(left, right, (((1,), (0,)), ((), ())), preferred_element_type=F32)


def complex_block(re, im):
    return jnp.concatenate(
        [jnp.concatenate([re, im], axis=1), jnp.concatenate([-im, re], axis=1)], axis=0
    )


def kernel(
    n, nt, chunk, turned,
    mom_hbm, sink_hbm, pick_hbm, time_hbm, vec_hbm, per_hbm,
    out_ref,
    mom_ref, sink_ref, pick_ref, time_ref,
    ab, trans, trig, acc, per, part, rx1, s1, rx2, full, tabuf, src, half,
    int_sem, vec_sem, per_sem, ta_s, ta_r, sl_s, sl_r,
    x1_s, x1_r, x2_s, x2_r, x3_s, x3_r,
):
    nmom = part.shape[0]
    rank = part.shape[-1]
    colours, sites = ab.shape[0], ab.shape[1]
    blocks = out_ref.shape[1]
    rows = rank // n
    hrows = rank // 2
    g = lax.axis_index("gx")
    t = lax.axis_index("ta")
    core = lax.rem(g, 2)
    partner = g + 1 - 2 * core
    chips = n // 2

    def ahead(d):
        return lax.rem(g + d, n)

    def remote(src_ref, dst_ref, ss, rs, **where):
        return pltpu.make_async_remote_copy(
            src_ref=src_ref, dst_ref=dst_ref, send_sem=ss, recv_sem=rs,
            device_id=where, device_id_type=MESH,
        )

    integers = [
        pltpu.make_async_copy(where, to, int_sem.at[i])
        for i, (where, to) in enumerate(
            [(mom_hbm, mom_ref), (sink_hbm, sink_ref), (pick_hbm, pick_ref), (time_hbm, time_ref)]
        )
    ]
    for load in integers:
        load.start()
    barrier = pltpu.get_barrier_semaphore()
    for d in range(1, n):
        pl.semaphore_signal(barrier, inc=1, device_id={"gx": ahead(d)}, device_id_type=MESH)
    for d in range(1, nt):
        pl.semaphore_signal(
            barrier, inc=1, device_id={"ta": lax.rem(t + d, nt)}, device_id_type=MESH
        )

    loads = []
    for col in range(colours):
        for ri in range(2):
            load = pltpu.make_async_copy(
                vec_hbm.at[0, ri, col],
                ab.at[col, :, pl.ds(ri * rank, rank)],
                vec_sem.at[col, ri],
            )
            load.start()
            loads.append(load)
    per_load = pltpu.make_async_copy(per_hbm.at[0], per, per_sem)
    per_load.start()

    for load in integers:
        load.wait()

    slab_x = sites // (LY * LZ)
    shape = (8, sites)
    row = lax.broadcasted_iota(jnp.int32, shape, 0)
    site = lax.broadcasted_iota(jnp.int32, shape, 1)

    def component(axis):
        value = jnp.zeros(shape, F32)
        for m in range(nmom):
            value = jnp.where(row == m, mom_ref[m, axis].astype(F32), value)
        return value

    x = (g * slab_x + lax.shift_right_logical(site, int(math.log2(LY * LZ)))).astype(F32)
    y = (lax.shift_right_logical(site, int(math.log2(LZ))) & (LY - 1)).astype(F32)
    z = (site & (LZ - 1)).astype(F32)
    turns = (
        component(0) * x * (1.0 / (slab_x * n))
        + component(1) * y * (1.0 / LY)
        + component(2) * z * (1.0 / LZ)
    )
    turns = turns - jnp.floor(turns + 0.5)
    angle = (2.0 * math.pi) * turns
    trig[0] = jnp.cos(angle)
    trig[1] = jnp.sin(angle)

    scale = 1.0 / math.sqrt(colours * sites * n)

    def accumulate(p, col):
        for i in range(sites // chunk):
            at = slice(i * chunk, (i + 1) * chunk)
            a = trans[col, 0, :, at]
            b = trans[col, 1, :, at]
            c = trig[0, p : p + 1, at]
            s = trig[1, p : p + 1, at]
            for k, phased in enumerate((a * c + b * s, b * c - a * s)):
                product = mxu(phased.astype(BF16), ab[col, at, :])
                if col == 0 and i == 0:
                    acc[k] = product
                else:
                    acc[k] += product

    def finish(p):
        part[p, 0] = (acc[0, :, :rank] + acc[1, :, rank:]).T * scale
        part[p, 1] = (acc[1, :, :rank] - acc[0, :, rank:]).T * scale

    def band(at, size):
        return pl.ds(pl.multiple_of(at * size, size), size)

    mine = pl.ds(pl.multiple_of(core * hrows + lax.div(g, 2) * rows, rows), rows)
    sends = []

    def ta_copy(d):
        return remote(
            tabuf.at[t], tabuf.at[t], ta_s.at[d - 1], ta_r.at[d - 1], ta=lax.rem(t + d, nt)
        )

    def sl_copy(d):
        return remote(
            src.at[:, mine], src.at[:, mine], sl_s.at[d - 1], sl_r.at[d - 1], gx=ahead(d)
        )

    def x1_copy(p):
        return remote(
            part.at[p, :, band(1 - core, hrows)], rx1.at[p], x1_s.at[p], x1_r.at[p],
            gx=partner,
        )

    def x2_copy(p, d):
        return remote(
            s1.at[p], rx2.at[p, d - 1], x2_s.at[p, d - 1], x2_r.at[p, d - 1],
            gx=ahead(2 * d),
        )

    def x3_copy(p):
        keep = full.at[p, :, band(core, hrows)]
        return remote(keep, keep, x3_s.at[p], x3_r.at[p], gx=partner)

    def go(copy):
        copy.start()
        sends.append(copy)

    def p0_select():
        for d in range(1, nt):
            ta_copy(d).wait_recv()
        root = lax.rem(time_ref[0], nt)
        src[:, mine] = tabuf[root]
        for d in range(1, n):
            go(sl_copy(d))

    def step2(p):
        x1_copy(p).wait_recv()
        s1[p] = part[p, :, band(core, hrows)] + rx1[p]
        for d in range(1, chips):
            go(x2_copy(p, d))

    def step3(p):
        total = s1[p]
        for d in range(1, chips):
            x2_copy(p, d).wait_recv()
            total = total + rx2[p, d - 1]
        full[p, :, band(core, hrows)] = total
        if p == 0:
            tabuf[t] = full[0, :, mine]
            for d in range(1, nt):
                go(ta_copy(d))
        go(x3_copy(p))

    eye = jnp.where(
        lax.broadcasted_iota(jnp.int32, (2 * rank, 2 * rank), 0)
        == lax.broadcasted_iota(jnp.int32, (2 * rank, 2 * rank), 1),
        1.0, 0.0,
    ).astype(BF16)
    def turn(col):
        loads[2 * col].wait()
        loads[2 * col + 1].wait()
        for ri in range(2):
            trans[col, ri, :, :turned] = ab[col, :turned, ri * rank : (ri + 1) * rank].astype(F32).T
        if turned < sites:
            rest = lax.dot_general(
                eye, ab[col, turned:, :], (((1,), (1,)), ((), ())), preferred_element_type=F32
            )
            trans[col, 0, :, turned:] = rest[:rank]
            trans[col, 1, :, turned:] = rest[rank:]

    turn(0)
    for col in range(colours):
        if col + 1 < colours:
            turn(col + 1)
        accumulate(0, col)
    finish(0)
    pl.semaphore_wait(barrier, n + nt - 2)
    go(x1_copy(0))
    for p in range(1, nmom):
        for col in range(colours):
            accumulate(p, col)
        step2(p - 1)
        finish(p)
        go(x1_copy(p))
    step2(nmom - 1)
    for p in range(nmom):
        step3(p)
    p0_select()

    per_load.wait()
    for p in range(nmom):
        x3_copy(p).wait_recv()
    for j in range(blocks):
        sink = sink_ref[g * blocks + j]
        pick = pick_ref[g * blocks + j]
        e_high, e_low = split(jnp.concatenate([full[sink, 0], full[sink, 1]], axis=1))
        spin = complex_block(per[pick, 0], per[pick, 1])
        half[j * rank : (j + 1) * rank] = mxu(e_high, spin) + mxu(e_low, spin)
    h_high, h_low = split(half[...] * (1.0 / math.sqrt(rank)))
    for d in range(1, n):
        sl_copy(d).wait_recv()
    s_high, s_low = split(complex_block(src[0], src[1]))
    for j in range(blocks):
        at = slice(j * rank, (j + 1) * rank)
        corr = mxu(h_high[at], s_high) + mxu(h_high[at], s_low) + mxu(h_low[at], s_high)
        out_ref[0, j, 0] = corr[:, :rank]
        out_ref[0, j, 1] = corr[:, rank:]
    for copy in sends:
        copy.wait_send()


def in_hbm(array):
    return pltpu.with_memory_space_constraint(array, pltpu.HBM)


def body(vectors, peramb, momenta, sink_mom, spin_pick, src_time):
    n = lax.axis_size("gx")
    nt = lax.axis_size("ta")
    colours, sites, rank = vectors.shape[2:]
    nmom = momenta.shape[0]
    spins = sink_mom.shape[0]
    blocks = spins // n
    rows = rank // n
    chips = n // 2
    chunk = min(1024, sites)
    turned = sites * 7 // 8 // 256 * 256
    dma = pltpu.SemaphoreType.DMA
    hbm = pl.BlockSpec(memory_space=pl.ANY)
    return pl.pallas_call(
        functools.partial(kernel, n, nt, chunk, turned),
        out_shape=pltpu.VMEM((1, blocks, 2, rank, rank), F32),
        in_specs=[hbm] * 6,
        out_specs=pl.BlockSpec(memory_space=pltpu.VMEM),
        scratch_shapes=[
            pltpu.SMEM(momenta.shape, jnp.int32),
            pltpu.SMEM(sink_mom.shape, jnp.int32),
            pltpu.SMEM(spin_pick.shape, jnp.int32),
            pltpu.SMEM(src_time.shape, jnp.int32),
            pltpu.VMEM((colours, sites, 2 * rank), BF16),
            pltpu.VMEM((colours, 2, rank, sites), F32),
            pltpu.VMEM((2, 8, sites), F32),
            pltpu.VMEM((2, rank, 2 * rank), F32),
            pltpu.VMEM(peramb.shape[1:], BF16),
            pltpu.VMEM((nmom, 2, rank, rank), F32),
            pltpu.VMEM((nmom, 2, rank // 2, rank), F32),
            pltpu.VMEM((nmom, 2, rank // 2, rank), F32),
            pltpu.VMEM((nmom, max(chips - 1, 1), 2, rank // 2, rank), F32),
            pltpu.VMEM((nmom, 2, rank, rank), F32),
            pltpu.VMEM((nt, 2, rows, rank), F32),
            pltpu.VMEM((2, rank, rank), F32),
            pltpu.VMEM((blocks * rank, 2 * rank), F32),
            dma((4,)),
            dma((colours, 2)),
            dma,
            dma((max(nt - 1, 1),)), dma((max(nt - 1, 1),)),
            dma((n - 1,)), dma((n - 1,)),
            dma((nmom,)), dma((nmom,)),
            dma((nmom, max(chips - 1, 1))), dma((nmom, max(chips - 1, 1))),
            dma((nmom,)), dma((nmom,)),
        ],
        compiler_params=pltpu.CompilerParams(
            collective_id=0, has_side_effects=True, vmem_limit_bytes=50*2**20
        ),
    )(
        in_hbm(momenta), in_hbm(sink_mom), in_hbm(spin_pick), src_time,
        in_hbm(vectors), in_hbm(peramb),
    )


def solution(mesh):
    placed = (
        P(("grp", "ta"), None, None, "gx", None),
        P(("grp", "ta"), None, None, None, None),
        P("grp", None),
        P("grp"),
        P("grp"),
        P("grp"),
    )
    return jax.shard_map(
        body,
        mesh=mesh,
        in_specs=placed,
        out_specs=P(("grp", "ta"), "gx", None, None, None),
        check_vma=False,
    )
```

```python
import functools
import math

import jax
import jax.numpy as jnp
from jax import lax
from jax.experimental import pallas as pl
from jax.experimental.pallas import tpu as pltpu
from jax.sharding import PartitionSpec as P

LY = 32
LZ = 32
MESH = pl.DeviceIdType.MESH
F32 = jnp.float32
BF16 = jnp.bfloat16


def split(value):
    high = value.astype(BF16)
    low = (value - high.astype(F32)).astype(BF16)
    return high, low


def mxu(left, right):
    return lax.dot_general(left, right, (((1,), (0,)), ((), ())), preferred_element_type=F32)


def complex_block(re, im):
    return jnp.concatenate(
        [jnp.concatenate([re, im], axis=1), jnp.concatenate([-im, re], axis=1)], axis=0
    )


def kernel(
    n, nt, chunk, turned,
    mom_hbm, sink_hbm, pick_hbm, time_hbm, vec_hbm, per_hbm,
    out_ref,
    mom_ref, sink_ref, pick_ref, time_ref,
    ab, trans, trig, acc, per, part, rxq, rx1, s1, rx2, full, tabuf, src, half,
    int_sem, vec_sem, per_sem, rs_s, rs_r, ta_s, ta_r, sl_s, sl_r,
    x1_s, x1_r, x2_s, x2_r, x3_s, x3_r,
):
    nmom = part.shape[0]
    rank = part.shape[-1]
    colours, sites = ab.shape[0], ab.shape[1]
    blocks = out_ref.shape[1]
    rows = rank // n
    hrows = rank // 2
    g = lax.axis_index("gx")
    t = lax.axis_index("ta")
    core = lax.rem(g, 2)
    partner = g + 1 - 2 * core
    chips = n // 2

    def ahead(d):
        return lax.rem(g + d, n)

    def remote(src_ref, dst_ref, ss, rs, **where):
        return pltpu.make_async_remote_copy(
            src_ref=src_ref, dst_ref=dst_ref, send_sem=ss, recv_sem=rs,
            device_id=where, device_id_type=MESH,
        )

    integers = [
        pltpu.make_async_copy(where, to, int_sem.at[i])
        for i, (where, to) in enumerate(
            [(mom_hbm, mom_ref), (sink_hbm, sink_ref), (pick_hbm, pick_ref), (time_hbm, time_ref)]
        )
    ]
    for load in integers:
        load.start()
    barrier = pltpu.get_barrier_semaphore()
    for d in range(1, n):
        pl.semaphore_signal(barrier, inc=1, device_id={"gx": ahead(d)}, device_id_type=MESH)
    for d in range(1, nt):
        pl.semaphore_signal(
            barrier, inc=1, device_id={"ta": lax.rem(t + d, nt)}, device_id_type=MESH
        )

    loads = []
    for col in range(colours):
        for ri in range(2):
            load = pltpu.make_async_copy(
                vec_hbm.at[0, ri, col],
                ab.at[col, :, pl.ds(ri * rank, rank)],
                vec_sem.at[col, ri],
            )
            load.start()
            loads.append(load)
    per_load = pltpu.make_async_copy(per_hbm.at[0], per, per_sem)
    per_load.start()

    for load in integers:
        load.wait()

    slab_x = sites // (LY * LZ)
    shape = (8, sites)
    row = lax.broadcasted_iota(jnp.int32, shape, 0)
    site = lax.broadcasted_iota(jnp.int32, shape, 1)

    def component(axis):
        value = jnp.zeros(shape, F32)
        for m in range(nmom):
            value = jnp.where(row == m, mom_ref[m, axis].astype(F32), value)
        return value

    x = (g * slab_x + lax.shift_right_logical(site, int(math.log2(LY * LZ)))).astype(F32)
    y = (lax.shift_right_logical(site, int(math.log2(LZ))) & (LY - 1)).astype(F32)
    z = (site & (LZ - 1)).astype(F32)
    turns = (
        component(0) * x * (1.0 / (slab_x * n))
        + component(1) * y * (1.0 / LY)
        + component(2) * z * (1.0 / LZ)
    )
    turns = turns - jnp.floor(turns + 0.5)
    angle = (2.0 * math.pi) * turns
    trig[0] = jnp.cos(angle)
    trig[1] = jnp.sin(angle)

    scale = 1.0 / math.sqrt(colours * sites * n)

    def accumulate(p, col):
        for i in range(sites // chunk):
            at = slice(i * chunk, (i + 1) * chunk)
            a = trans[col, 0, :, at]
            b = trans[col, 1, :, at]
            c = trig[0, p : p + 1, at]
            s = trig[1, p : p + 1, at]
            for k, phased in enumerate((a * c + b * s, b * c - a * s)):
                product = mxu(phased.astype(BF16), ab[col, at, :])
                if col == 0 and i == 0:
                    acc[k] = product
                else:
                    acc[k] += product

    def finish(p):
        part[p, 0] = (acc[0, :, :rank] + acc[1, :, rank:]).T * scale
        part[p, 1] = (acc[1, :, :rank] - acc[0, :, rank:]).T * scale

    def band(at, size):
        return pl.ds(pl.multiple_of(at * size, size), size)

    sends = []

    def quarter(owner):
        at = lax.rem(owner, 2) * hrows + lax.div(owner, 2) * rows
        return pl.ds(pl.multiple_of(at, rows), rows)

    def rs_copy(d):
        return remote(
            part.at[0, :, quarter(ahead(d))], rxq.at[d - 1], rs_s.at[d - 1], rs_r.at[d - 1],
            gx=ahead(d),
        )

    def ta_copy(d):
        return remote(
            tabuf.at[t], tabuf.at[t], ta_s.at[d - 1], ta_r.at[d - 1], ta=lax.rem(t + d, nt)
        )

    def sl_copy(d):
        return remote(
            src.at[:, mine], src.at[:, mine], sl_s.at[d - 1], sl_r.at[d - 1], gx=ahead(d)
        )

    def x1_copy(p):
        return remote(
            part.at[p, :, band(1 - core, hrows)], rx1.at[p], x1_s.at[p], x1_r.at[p],
            gx=partner,
        )

    def x2_copy(p, d):
        return remote(
            s1.at[p], rx2.at[p, d - 1], x2_s.at[p, d - 1], x2_r.at[p, d - 1],
            gx=ahead(2 * d),
        )

    def x3_copy(p):
        keep = full.at[p, :, band(core, hrows)]
        return remote(keep, keep, x3_s.at[p], x3_r.at[p], gx=partner)

    def go(copy):
        copy.start()
        sends.append(copy)

    mine = quarter(g)

    def p0_scatter():
        total = part[0, :, mine]
        for d in range(1, n):
            rs_copy(d).wait_recv()
            total = total + rxq[d - 1]
        tabuf[t] = total
        for d in range(1, nt):
            go(ta_copy(d))

    def p0_select():
        for d in range(1, nt):
            ta_copy(d).wait_recv()
        root = lax.rem(time_ref[0], nt)
        src[:, mine] = tabuf[root]
        for d in range(1, n):
            go(sl_copy(d))

    def step2(p):
        x1_copy(p).wait_recv()
        s1[p] = part[p, :, band(core, hrows)] + rx1[p]
        for d in range(1, chips):
            go(x2_copy(p, d))

    def step3(p):
        total = s1[p]
        for d in range(1, chips):
            x2_copy(p, d).wait_recv()
            total = total + rx2[p, d - 1]
        full[p, :, band(core, hrows)] = total
        go(x3_copy(p))

    eye = jnp.where(
        lax.broadcasted_iota(jnp.int32, (2 * rank, 2 * rank), 0)
        == lax.broadcasted_iota(jnp.int32, (2 * rank, 2 * rank), 1),
        1.0, 0.0,
    ).astype(BF16)
    def turn(col):
        loads[2 * col].wait()
        loads[2 * col + 1].wait()
        for ri in range(2):
            trans[col, ri, :, :turned] = ab[col, :turned, ri * rank : (ri + 1) * rank].astype(F32).T
        if turned < sites:
            rest = lax.dot_general(
                eye, ab[col, turned:, :], (((1,), (1,)), ((), ())), preferred_element_type=F32
            )
            trans[col, 0, :, turned:] = rest[:rank]
            trans[col, 1, :, turned:] = rest[rank:]

    turn(0)
    for col in range(colours):
        if col + 1 < colours:
            turn(col + 1)
        accumulate(0, col)
    finish(0)
    pl.semaphore_wait(barrier, n + nt - 2)
    for d in range(1, n):
        go(rs_copy(d))
    go(x1_copy(0))
    for p in range(1, nmom):
        for col in range(colours):
            accumulate(p, col)
        step2(p - 1)
        finish(p)
        go(x1_copy(p))
    p0_scatter()
    step2(nmom - 1)
    for p in range(nmom - 1):
        step3(p)
    p0_select()
    step3(nmom - 1)

    per_load.wait()
    for p in range(nmom):
        x3_copy(p).wait_recv()
    for j in range(blocks):
        sink = sink_ref[g * blocks + j]
        pick = pick_ref[g * blocks + j]
        e_high, e_low = split(jnp.concatenate([full[sink, 0], full[sink, 1]], axis=1))
        spin = complex_block(per[pick, 0], per[pick, 1])
        half[j * rank : (j + 1) * rank] = mxu(e_high, spin) + mxu(e_low, spin)
    h_high, h_low = split(half[...] * (1.0 / math.sqrt(rank)))
    for d in range(1, n):
        sl_copy(d).wait_recv()
    s_high, s_low = split(complex_block(src[0], src[1]))
    for j in range(blocks):
        at = slice(j * rank, (j + 1) * rank)
        corr = mxu(h_high[at], s_high) + mxu(h_high[at], s_low) + mxu(h_low[at], s_high)
        out_ref[0, j, 0] = corr[:, :rank]
        out_ref[0, j, 1] = corr[:, rank:]
    for copy in sends:
        copy.wait_send()


def in_hbm(array):
    return pltpu.with_memory_space_constraint(array, pltpu.HBM)


def body(vectors, peramb, momenta, sink_mom, spin_pick, src_time):
    n = lax.axis_size("gx")
    nt = lax.axis_size("ta")
    colours, sites, rank = vectors.shape[2:]
    nmom = momenta.shape[0]
    spins = sink_mom.shape[0]
    blocks = spins // n
    rows = rank // n
    chips = n // 2
    chunk = min(1024, sites)
    turned = sites * 7 // 8 // 256 * 256
    dma = pltpu.SemaphoreType.DMA
    hbm = pl.BlockSpec(memory_space=pl.ANY)
    return pl.pallas_call(
        functools.partial(kernel, n, nt, chunk, turned),
        out_shape=pltpu.VMEM((1, blocks, 2, rank, rank), F32),
        in_specs=[hbm] * 6,
        out_specs=pl.BlockSpec(memory_space=pltpu.VMEM),
        scratch_shapes=[
            pltpu.SMEM(momenta.shape, jnp.int32),
            pltpu.SMEM(sink_mom.shape, jnp.int32),
            pltpu.SMEM(spin_pick.shape, jnp.int32),
            pltpu.SMEM(src_time.shape, jnp.int32),
            pltpu.VMEM((colours, sites, 2 * rank), BF16),
            pltpu.VMEM((colours, 2, rank, sites), F32),
            pltpu.VMEM((2, 8, sites), F32),
            pltpu.VMEM((2, rank, 2 * rank), F32),
            pltpu.VMEM(peramb.shape[1:], BF16),
            pltpu.VMEM((nmom, 2, rank, rank), F32),
            pltpu.VMEM((n - 1, 2, rows, rank), F32),
            pltpu.VMEM((nmom, 2, rank // 2, rank), F32),
            pltpu.VMEM((nmom, 2, rank // 2, rank), F32),
            pltpu.VMEM((nmom, max(chips - 1, 1), 2, rank // 2, rank), F32),
            pltpu.VMEM((nmom, 2, rank, rank), F32),
            pltpu.VMEM((nt, 2, rows, rank), F32),
            pltpu.VMEM((2, rank, rank), F32),
            pltpu.VMEM((blocks * rank, 2 * rank), F32),
            dma((4,)),
            dma((colours, 2)),
            dma,
            dma((n - 1,)), dma((n - 1,)),
            dma((max(nt - 1, 1),)), dma((max(nt - 1, 1),)),
            dma((n - 1,)), dma((n - 1,)),
            dma((nmom,)), dma((nmom,)),
            dma((nmom, max(chips - 1, 1))), dma((nmom, max(chips - 1, 1))),
            dma((nmom,)), dma((nmom,)),
        ],
        compiler_params=pltpu.CompilerParams(
            collective_id=0, has_side_effects=True, vmem_limit_bytes=50*2**20
        ),
    )(
        in_hbm(momenta), in_hbm(sink_mom), in_hbm(spin_pick), src_time,
        in_hbm(vectors), in_hbm(peramb),
    )


def solution(mesh):
    placed = (
        P(("grp", "ta"), None, None, "gx", None),
        P(("grp", "ta"), None, None, None, None),
        P("grp", None),
        P("grp"),
        P("grp"),
        P("grp"),
    )
    return jax.shard_map(
        body,
        mesh=mesh,
        in_specs=placed,
        out_specs=P(("grp", "ta"), "gx", None, None, None),
        check_vma=False,
    )
```

```python
import functools
import math

import jax
import jax.numpy as jnp
from jax import lax
from jax.experimental import pallas as pl
from jax.experimental.pallas import tpu as pltpu
from jax.sharding import PartitionSpec as P

LY = 32
LZ = 32
MESH = pl.DeviceIdType.MESH
F32 = jnp.float32
BF16 = jnp.bfloat16


def split(value):
    high = value.astype(BF16)
    low = (value - high.astype(F32)).astype(BF16)
    return high, low


def mxu(left, right):
    return lax.dot_general(left, right, (((1,), (0,)), ((), ())), preferred_element_type=F32)


def complex_block(re, im):
    return jnp.concatenate(
        [jnp.concatenate([re, im], axis=1), jnp.concatenate([-im, re], axis=1)], axis=0
    )


def kernel(
    n, nt, chunk,
    mom_hbm, sink_hbm, pick_hbm, time_hbm, vec_hbm, per_hbm,
    out_ref,
    mom_ref, sink_ref, pick_ref, time_ref,
    ab, trans, trig, acc, per, part, rxq, rx1, s1, rx2, full, tabuf, src, half,
    int_sem, vec_sem, per_sem, rs_s, rs_r, ta_s, ta_r, sl_s, sl_r,
    x1_s, x1_r, x2_s, x2_r, x3_s, x3_r,
):
    nmom = part.shape[0]
    rank = part.shape[-1]
    colours, sites = ab.shape[0], ab.shape[1]
    blocks = out_ref.shape[1]
    rows = rank // n
    hrows = rank // 2
    g = lax.axis_index("gx")
    t = lax.axis_index("ta")
    core = lax.rem(g, 2)
    partner = g + 1 - 2 * core
    chips = n // 2

    def ahead(d):
        return lax.rem(g + d, n)

    def remote(src_ref, dst_ref, ss, rs, **where):
        return pltpu.make_async_remote_copy(
            src_ref=src_ref, dst_ref=dst_ref, send_sem=ss, recv_sem=rs,
            device_id=where, device_id_type=MESH,
        )

    integers = [
        pltpu.make_async_copy(where, to, int_sem.at[i])
        for i, (where, to) in enumerate(
            [(mom_hbm, mom_ref), (sink_hbm, sink_ref), (pick_hbm, pick_ref), (time_hbm, time_ref)]
        )
    ]
    for load in integers:
        load.start()
    barrier = pltpu.get_barrier_semaphore()
    for d in range(1, n):
        pl.semaphore_signal(barrier, inc=1, device_id={"gx": ahead(d)}, device_id_type=MESH)
    for d in range(1, nt):
        pl.semaphore_signal(
            barrier, inc=1, device_id={"ta": lax.rem(t + d, nt)}, device_id_type=MESH
        )

    loads = []
    for col in range(colours):
        for ri in range(2):
            load = pltpu.make_async_copy(
                vec_hbm.at[0, ri, col],
                ab.at[col, :, pl.ds(ri * rank, rank)],
                vec_sem.at[col, ri],
            )
            load.start()
            loads.append(load)
    per_load = pltpu.make_async_copy(per_hbm.at[0], per, per_sem)
    per_load.start()

    for load in integers:
        load.wait()

    slab_x = sites // (LY * LZ)
    shape = (8, sites)
    row = lax.broadcasted_iota(jnp.int32, shape, 0)
    site = lax.broadcasted_iota(jnp.int32, shape, 1)

    def component(axis):
        value = jnp.zeros(shape, F32)
        for m in range(nmom):
            value = jnp.where(row == m, mom_ref[m, axis].astype(F32), value)
        return value

    x = (g * slab_x + lax.shift_right_logical(site, int(math.log2(LY * LZ)))).astype(F32)
    y = (lax.shift_right_logical(site, int(math.log2(LZ))) & (LY - 1)).astype(F32)
    z = (site & (LZ - 1)).astype(F32)
    turns = (
        component(0) * x * (1.0 / (slab_x * n))
        + component(1) * y * (1.0 / LY)
        + component(2) * z * (1.0 / LZ)
    )
    turns = turns - jnp.floor(turns + 0.5)
    angle = (2.0 * math.pi) * turns
    trig[0] = jnp.cos(angle)
    trig[1] = jnp.sin(angle)

    scale = 1.0 / math.sqrt(colours * sites * n)

    def accumulate(p, col):
        for i in range(sites // chunk):
            at = slice(i * chunk, (i + 1) * chunk)
            a = trans[col, 0, :, at]
            b = trans[col, 1, :, at]
            c = trig[0, p : p + 1, at]
            s = trig[1, p : p + 1, at]
            for k, phased in enumerate((a * c + b * s, b * c - a * s)):
                product = mxu(phased.astype(BF16), ab[col, at, :])
                if col == 0 and i == 0:
                    acc[k] = product
                else:
                    acc[k] += product

    def finish(p):
        part[p, 0] = (acc[0, :, :rank] + acc[1, :, rank:]).T * scale
        part[p, 1] = (acc[1, :, :rank] - acc[0, :, rank:]).T * scale

    def band(at, size):
        return pl.ds(pl.multiple_of(at * size, size), size)

    sends = []

    def quarter(owner):
        at = lax.rem(owner, 2) * hrows + lax.div(owner, 2) * rows
        return pl.ds(pl.multiple_of(at, rows), rows)

    def rs_copy(d):
        return remote(
            part.at[0, :, quarter(ahead(d))], rxq.at[d - 1], rs_s.at[d - 1], rs_r.at[d - 1],
            gx=ahead(d),
        )

    def ta_copy(d):
        return remote(
            tabuf.at[t], tabuf.at[t], ta_s.at[d - 1], ta_r.at[d - 1], ta=lax.rem(t + d, nt)
        )

    def sl_copy(d):
        return remote(
            src.at[:, mine], src.at[:, mine], sl_s.at[d - 1], sl_r.at[d - 1], gx=ahead(d)
        )

    def x1_copy(p):
        return remote(
            part.at[p, :, band(1 - core, hrows)], rx1.at[p], x1_s.at[p], x1_r.at[p],
            gx=partner,
        )

    def x2_copy(p, d):
        return remote(
            s1.at[p], rx2.at[p, d - 1], x2_s.at[p, d - 1], x2_r.at[p, d - 1],
            gx=ahead(2 * d),
        )

    def x3_copy(p):
        keep = full.at[p, :, band(core, hrows)]
        return remote(keep, keep, x3_s.at[p], x3_r.at[p], gx=partner)

    def go(copy):
        copy.start()
        sends.append(copy)

    mine = quarter(g)

    def p0_scatter():
        total = part[0, :, mine]
        for d in range(1, n):
            rs_copy(d).wait_recv()
            total = total + rxq[d - 1]
        tabuf[t] = total
        for d in range(1, nt):
            go(ta_copy(d))

    def p0_select():
        for d in range(1, nt):
            ta_copy(d).wait_recv()
        root = lax.rem(time_ref[0], nt)
        src[:, mine] = tabuf[root]
        for d in range(1, n):
            go(sl_copy(d))

    def step2(p):
        x1_copy(p).wait_recv()
        s1[p] = part[p, :, band(core, hrows)] + rx1[p]
        for d in range(1, chips):
            go(x2_copy(p, d))

    def step3(p):
        total = s1[p]
        for d in range(1, chips):
            x2_copy(p, d).wait_recv()
            total = total + rx2[p, d - 1]
        full[p, :, band(core, hrows)] = total
        go(x3_copy(p))

    for col in range(colours):
        loads[2 * col].wait()
        loads[2 * col + 1].wait()
        for ri in range(2):
            trans[col, ri] = ab[col, :, ri * rank : (ri + 1) * rank].T.astype(F32)
        accumulate(0, col)
    finish(0)
    pl.semaphore_wait(barrier, n + nt - 2)
    for d in range(1, n):
        go(rs_copy(d))
    go(x1_copy(0))
    for p in range(1, nmom):
        for col in range(colours):
            accumulate(p, col)
        step2(p - 1)
        finish(p)
        go(x1_copy(p))
    p0_scatter()
    step2(nmom - 1)
    for p in range(nmom - 1):
        step3(p)
    p0_select()
    step3(nmom - 1)

    per_load.wait()
    for p in range(nmom):
        x3_copy(p).wait_recv()
    for j in range(blocks):
        sink = sink_ref[g * blocks + j]
        pick = pick_ref[g * blocks + j]
        e_high, e_low = split(jnp.concatenate([full[sink, 0], full[sink, 1]], axis=1))
        spin = complex_block(per[pick, 0], per[pick, 1])
        half[j * rank : (j + 1) * rank] = mxu(e_high, spin) + mxu(e_low, spin)
    h_high, h_low = split(half[...] * (1.0 / math.sqrt(rank)))
    for d in range(1, n):
        sl_copy(d).wait_recv()
    s_high, s_low = split(complex_block(src[0], src[1]))
    for j in range(blocks):
        at = slice(j * rank, (j + 1) * rank)
        corr = mxu(h_high[at], s_high) + mxu(h_high[at], s_low) + mxu(h_low[at], s_high)
        out_ref[0, j, 0] = corr[:, :rank]
        out_ref[0, j, 1] = corr[:, rank:]
    for copy in sends:
        copy.wait_send()


def in_hbm(array):
    return pltpu.with_memory_space_constraint(array, pltpu.HBM)


def body(vectors, peramb, momenta, sink_mom, spin_pick, src_time):
    n = lax.axis_size("gx")
    nt = lax.axis_size("ta")
    colours, sites, rank = vectors.shape[2:]
    nmom = momenta.shape[0]
    spins = sink_mom.shape[0]
    blocks = spins // n
    rows = rank // n
    chips = n // 2
    chunk = min(1024, sites)
    dma = pltpu.SemaphoreType.DMA
    hbm = pl.BlockSpec(memory_space=pl.ANY)
    return pl.pallas_call(
        functools.partial(kernel, n, nt, chunk),
        out_shape=pltpu.VMEM((1, blocks, 2, rank, rank), F32),
        in_specs=[hbm] * 6,
        out_specs=pl.BlockSpec(memory_space=pltpu.VMEM),
        scratch_shapes=[
            pltpu.SMEM(momenta.shape, jnp.int32),
            pltpu.SMEM(sink_mom.shape, jnp.int32),
            pltpu.SMEM(spin_pick.shape, jnp.int32),
            pltpu.SMEM(src_time.shape, jnp.int32),
            pltpu.VMEM((colours, sites, 2 * rank), BF16),
            pltpu.VMEM((colours, 2, rank, sites), F32),
            pltpu.VMEM((2, 8, sites), F32),
            pltpu.VMEM((2, rank, 2 * rank), F32),
            pltpu.VMEM(peramb.shape[1:], BF16),
            pltpu.VMEM((nmom, 2, rank, rank), F32),
            pltpu.VMEM((n - 1, 2, rows, rank), F32),
            pltpu.VMEM((nmom, 2, rank // 2, rank), F32),
            pltpu.VMEM((nmom, 2, rank // 2, rank), F32),
            pltpu.VMEM((nmom, max(chips - 1, 1), 2, rank // 2, rank), F32),
            pltpu.VMEM((nmom, 2, rank, rank), F32),
            pltpu.VMEM((nt, 2, rows, rank), F32),
            pltpu.VMEM((2, rank, rank), F32),
            pltpu.VMEM((blocks * rank, 2 * rank), F32),
            dma((4,)),
            dma((colours, 2)),
            dma,
            dma((n - 1,)), dma((n - 1,)),
            dma((max(nt - 1, 1),)), dma((max(nt - 1, 1),)),
            dma((n - 1,)), dma((n - 1,)),
            dma((nmom,)), dma((nmom,)),
            dma((nmom, max(chips - 1, 1))), dma((nmom, max(chips - 1, 1))),
            dma((nmom,)), dma((nmom,)),
        ],
        compiler_params=pltpu.CompilerParams(
            collective_id=0, has_side_effects=True, vmem_limit_bytes=50*2**20
        ),
    )(
        in_hbm(momenta), in_hbm(sink_mom), in_hbm(spin_pick), src_time,
        in_hbm(vectors), in_hbm(peramb),
    )


def solution(mesh):
    placed = (
        P(("grp", "ta"), None, None, "gx", None),
        P(("grp", "ta"), None, None, None, None),
        P("grp", None),
        P("grp"),
        P("grp"),
        P("grp"),
    )
    return jax.shard_map(
        body,
        mesh=mesh,
        in_specs=placed,
        out_specs=P(("grp", "ta"), "gx", None, None, None),
        check_vma=False,
    )
```

```python
import functools
import math

import jax
import jax.numpy as jnp
from jax import lax
from jax.experimental import pallas as pl
from jax.experimental.pallas import tpu as pltpu
from jax.sharding import PartitionSpec as P

LY = 32
LZ = 32
MESH = pl.DeviceIdType.MESH
F32 = jnp.float32
BF16 = jnp.bfloat16


def split(value):
    high = value.astype(BF16)
    low = (value - high.astype(F32)).astype(BF16)
    return high, low


def mxu(left, right):
    return lax.dot_general(left, right, (((1,), (0,)), ((), ())), preferred_element_type=F32)


def complex_block(re, im):
    return jnp.concatenate(
        [jnp.concatenate([re, im], axis=1), jnp.concatenate([-im, re], axis=1)], axis=0
    )


def kernel(
    n, nt, chunk,
    mom_hbm, sink_hbm, pick_hbm, time_hbm, vec_hbm, per_hbm,
    h_out, s_out,
    mom_ref, sink_ref, pick_ref, time_ref,
    ab, trans, trig, acc, per, part, rxq, rx1, s1, rx2, full, tabuf, src, half,
    int_sem, vec_sem, per_sem, rs_s, rs_r, ta_s, ta_r, sl_s, sl_r,
    x1_s, x1_r, x2_s, x2_r, x3_s, x3_r,
):
    nmom = part.shape[0]
    rank = part.shape[-1]
    colours, sites = ab.shape[0], ab.shape[1]
    blocks = h_out.shape[1] // rank
    rows = rank // n
    hrows = rank // 2
    g = lax.axis_index("gx")
    t = lax.axis_index("ta")
    core = lax.rem(g, 2)
    partner = g + 1 - 2 * core
    chips = n // 2

    def ahead(d):
        return lax.rem(g + d, n)

    def remote(src_ref, dst_ref, ss, rs, **where):
        return pltpu.make_async_remote_copy(
            src_ref=src_ref, dst_ref=dst_ref, send_sem=ss, recv_sem=rs,
            device_id=where, device_id_type=MESH,
        )

    integers = [
        pltpu.make_async_copy(where, to, int_sem.at[i])
        for i, (where, to) in enumerate(
            [(mom_hbm, mom_ref), (sink_hbm, sink_ref), (pick_hbm, pick_ref), (time_hbm, time_ref)]
        )
    ]
    for load in integers:
        load.start()
    barrier = pltpu.get_barrier_semaphore()
    for d in range(1, n):
        pl.semaphore_signal(barrier, inc=1, device_id={"gx": ahead(d)}, device_id_type=MESH)
    for d in range(1, nt):
        pl.semaphore_signal(
            barrier, inc=1, device_id={"ta": lax.rem(t + d, nt)}, device_id_type=MESH
        )

    lead = sites // 2
    pieces = [(0, 0, lead), (0, lead, sites)] + [(col, 0, sites) for col in range(1, colours)]
    loads = []
    for i, (col, lo, hi) in enumerate(pieces):
        for ri in range(2):
            load = pltpu.make_async_copy(
                vec_hbm.at[0, ri, col, lo:hi],
                ab.at[col, lo:hi, ri * rank : (ri + 1) * rank],
                vec_sem.at[i, ri],
            )
            load.start()
            loads.append(load)
    per_load = pltpu.make_async_copy(per_hbm.at[0], per, per_sem)
    per_load.start()

    for load in integers:
        load.wait()

    slab_x = sites // (LY * LZ)
    shape = (8, sites)
    row = lax.broadcasted_iota(jnp.int32, shape, 0)
    site = lax.broadcasted_iota(jnp.int32, shape, 1)

    def component(axis):
        value = jnp.zeros(shape, F32)
        for m in range(nmom):
            value = jnp.where(row == m, mom_ref[m, axis].astype(F32), value)
        return value

    x = (g * slab_x + lax.shift_right_logical(site, int(math.log2(LY * LZ)))).astype(F32)
    y = (lax.shift_right_logical(site, int(math.log2(LZ))) & (LY - 1)).astype(F32)
    z = (site & (LZ - 1)).astype(F32)
    turns = (
        component(0) * x * (1.0 / (slab_x * n))
        + component(1) * y * (1.0 / LY)
        + component(2) * z * (1.0 / LZ)
    )
    turns = turns - jnp.floor(turns + 0.5)
    angle = (2.0 * math.pi) * turns
    trig[0] = jnp.cos(angle)
    trig[1] = jnp.sin(angle)

    scale = 1.0 / math.sqrt(colours * sites * n)

    def accumulate(p, col, lo, hi):
        for i in range(lo, hi, chunk):
            at = slice(i, i + chunk)
            a = trans[col, 0, :, at]
            b = trans[col, 1, :, at]
            c = trig[0, p : p + 1, at]
            s = trig[1, p : p + 1, at]
            for k, phased in enumerate((a * c + b * s, b * c - a * s)):
                product = mxu(phased.astype(BF16), ab[col, at, :])
                if col == 0 and i == 0:
                    acc[k] = product
                else:
                    acc[k] += product

    def finish(p):
        part[p, 0] = (acc[0, :, :rank] + acc[1, :, rank:]).T * scale
        part[p, 1] = (acc[1, :, :rank] - acc[0, :, rank:]).T * scale

    def band(at, size):
        return pl.ds(pl.multiple_of(at * size, size), size)

    sends = []

    def quarter(owner):
        at = lax.rem(owner, 2) * hrows + lax.div(owner, 2) * rows
        return pl.ds(pl.multiple_of(at, rows), rows)

    mine = quarter(g)

    def rs_copy(d):
        return remote(
            part.at[0, :, quarter(ahead(d))], rxq.at[d - 1], rs_s.at[d - 1], rs_r.at[d - 1],
            gx=ahead(d),
        )

    def ta_copy(d):
        return remote(
            tabuf.at[t], tabuf.at[t], ta_s.at[d - 1], ta_r.at[d - 1], ta=lax.rem(t + d, nt)
        )

    def sl_copy(d):
        return remote(
            src.at[:, mine], src.at[:, mine], sl_s.at[d - 1], sl_r.at[d - 1], gx=ahead(d)
        )

    def x1_copy(p):
        return remote(
            part.at[p, :, band(1 - core, hrows)], rx1.at[p], x1_s.at[p], x1_r.at[p],
            gx=partner,
        )

    def x2_copy(p, d):
        return remote(
            s1.at[p], rx2.at[p, d - 1], x2_s.at[p, d - 1], x2_r.at[p, d - 1],
            gx=ahead(2 * d),
        )

    def sink_copy(d):
        rows_out = full.at[0, :, mine]
        return remote(
            rows_out, rows_out, x2_s.at[0, d - 1], x2_r.at[0, d - 1], gx=ahead(2 * d)
        )

    def x3_copy(p):
        keep = full.at[p, :, band(core, hrows)]
        return remote(keep, keep, x3_s.at[p], x3_r.at[p], gx=partner)

    def go(copy):
        copy.start()
        sends.append(copy)

    def p0_scatter():
        total = part[0, :, mine]
        for d in range(1, n):
            rs_copy(d).wait_recv()
            total = total + rxq[d - 1]
        tabuf[t] = total
        for d in range(1, nt):
            go(ta_copy(d))
        full[0, :, mine] = total
        for d in range(1, chips):
            go(sink_copy(d))

    def p0_select():
        for d in range(1, nt):
            ta_copy(d).wait_recv()
        root = lax.rem(time_ref[0], nt)
        src[:, mine] = tabuf[root]
        for d in range(1, n):
            go(sl_copy(d))

    def step2(p):
        x1_copy(p).wait_recv()
        s1[p] = part[p, :, band(core, hrows)] + rx1[p]
        for d in range(1, chips):
            go(x2_copy(p, d))

    def p0_sink():
        for d in range(1, chips):
            sink_copy(d).wait_recv()
        go(x3_copy(0))

    def step3(p):
        total = s1[p]
        for d in range(1, chips):
            x2_copy(p, d).wait_recv()
            total = total + rx2[p, d - 1]
        full[p, :, band(core, hrows)] = total
        go(x3_copy(p))

    for i, (col, lo, hi) in enumerate(pieces):
        loads[2 * i].wait()
        loads[2 * i + 1].wait()
        for ri in range(2):
            trans[col, ri, :, lo:hi] = ab[col, lo:hi, ri * rank : (ri + 1) * rank].T.astype(F32)
        accumulate(0, col, lo, hi)
    finish(0)
    pl.semaphore_wait(barrier, n + nt - 2)
    for d in range(1, n):
        go(rs_copy(d))
    for p in range(1, nmom):
        for col in range(colours):
            accumulate(p, col, 0, sites)
            if p > 2 and col == 0:
                step2(p - 2)
        if p == nmom - 1:
            p0_scatter()
            if p > 1:
                step2(p - 1)
        finish(p)
        go(x1_copy(p))
    if nmom > 1:
        step2(nmom - 1)
    else:
        p0_scatter()
    for p in range(1, nmom - 1):
        step3(p)
    p0_sink()
    p0_select()
    if nmom > 1:
        step3(nmom - 1)

    per_load.wait()
    for p in range(nmom):
        x3_copy(p).wait_recv()
    for j in range(blocks):
        sink = sink_ref[g * blocks + j]
        pick = pick_ref[g * blocks + j]
        e_high, e_low = split(jnp.concatenate([full[sink, 0], full[sink, 1]], axis=1))
        spin = complex_block(per[pick, 0], per[pick, 1])
        half[j * rank : (j + 1) * rank] = mxu(e_high, spin) + mxu(e_low, spin)
    h_out[0], h_out[1] = split(half[...] * (1.0 / math.sqrt(rank)))
    for d in range(1, n):
        sl_copy(d).wait_recv()
    s_out[0], s_out[1] = split(complex_block(src[0], src[1]))
    for copy in sends:
        copy.wait_send()


def close(h_ref, s_ref, out_hbm, outbuf, sems):
    blocks = outbuf.shape[0]
    rank = outbuf.shape[-1]
    stores = []
    for j in range(blocks):
        at = slice(j * rank, (j + 1) * rank)
        corr = (
            mxu(h_ref[0, at], s_ref[0]) + mxu(h_ref[0, at], s_ref[1]) + mxu(h_ref[1, at], s_ref[0])
        )
        outbuf[j, 0] = corr[:, :rank]
        outbuf[j, 1] = corr[:, rank:]
        store = pltpu.make_async_copy(outbuf.at[j], out_hbm.at[0, j], sems.at[j])
        store.start()
        stores.append(store)
    for store in stores:
        store.wait()


def in_hbm(array):
    return pltpu.with_memory_space_constraint(array, pltpu.HBM)


def body(vectors, peramb, momenta, sink_mom, spin_pick, src_time):
    n = lax.axis_size("gx")
    nt = lax.axis_size("ta")
    colours, sites, rank = vectors.shape[2:]
    nmom = momenta.shape[0]
    spins = sink_mom.shape[0]
    blocks = spins // n
    rows = rank // n
    chips = n // 2
    chunk = min(1024, sites // 2)
    dma = pltpu.SemaphoreType.DMA
    hbm = pl.BlockSpec(memory_space=pl.ANY)
    h, s = pl.pallas_call(
        functools.partial(kernel, n, nt, chunk),
        out_shape=(
            pltpu.VMEM((2, blocks * rank, 2 * rank), BF16),
            pltpu.VMEM((2, 2 * rank, 2 * rank), BF16),
        ),
        in_specs=[hbm] * 6,
        out_specs=(pl.BlockSpec(memory_space=pltpu.VMEM),) * 2,
        scratch_shapes=[
            pltpu.SMEM(momenta.shape, jnp.int32),
            pltpu.SMEM(sink_mom.shape, jnp.int32),
            pltpu.SMEM(spin_pick.shape, jnp.int32),
            pltpu.SMEM(src_time.shape, jnp.int32),
            pltpu.VMEM((colours, sites, 2 * rank), BF16),
            pltpu.VMEM((colours, 2, rank, sites), F32),
            pltpu.VMEM((2, 8, sites), F32),
            pltpu.VMEM((2, rank, 2 * rank), F32),
            pltpu.VMEM(peramb.shape[1:], BF16),
            pltpu.VMEM((nmom, 2, rank, rank), F32),
            pltpu.VMEM((n - 1, 2, rows, rank), F32),
            pltpu.VMEM((nmom, 2, rank // 2, rank), F32),
            pltpu.VMEM((nmom, 2, rank // 2, rank), F32),
            pltpu.VMEM((nmom, max(chips - 1, 1), 2, rank // 2, rank), F32),
            pltpu.VMEM((nmom, 2, rank, rank), F32),
            pltpu.VMEM((nt, 2, rows, rank), F32),
            pltpu.VMEM((2, rank, rank), F32),
            pltpu.VMEM((blocks * rank, 2 * rank), F32),
            dma((4,)),
            dma((colours + 1, 2)),
            dma,
            dma((n - 1,)), dma((n - 1,)),
            dma((max(nt - 1, 1),)), dma((max(nt - 1, 1),)),
            dma((n - 1,)), dma((n - 1,)),
            dma((nmom,)), dma((nmom,)),
            dma((nmom, max(chips - 1, 1))), dma((nmom, max(chips - 1, 1))),
            dma((nmom,)), dma((nmom,)),
        ],
        compiler_params=pltpu.CompilerParams(
            collective_id=0, has_side_effects=True, vmem_limit_bytes=50*2**20
        ),
    )(
        in_hbm(momenta), in_hbm(sink_mom), in_hbm(spin_pick), src_time,
        in_hbm(vectors), in_hbm(peramb),
    )
    return pl.pallas_call(
        close,
        out_shape=jax.ShapeDtypeStruct((1, blocks, 2, rank, rank), F32),
        in_specs=[pl.BlockSpec(memory_space=pltpu.VMEM)] * 2,
        out_specs=hbm,
        scratch_shapes=[pltpu.VMEM((blocks, 2, rank, rank), F32), dma((blocks,))],
        compiler_params=pltpu.CompilerParams(vmem_limit_bytes=8 * 2**20),
    )(h, s)


def solution(mesh):
    placed = (
        P(("grp", "ta"), None, None, "gx", None),
        P(("grp", "ta"), None, None, None, None),
        P("grp", None),
        P("grp"),
        P("grp"),
        P("grp"),
    )
    return jax.shard_map(
        body,
        mesh=mesh,
        in_specs=placed,
        out_specs=P(("grp", "ta"), "gx", None, None, None),
        check_vma=False,
    )
```

```python
import functools
import math

import jax
import jax.numpy as jnp
from jax import lax
from jax.experimental import pallas as pl
from jax.experimental.pallas import tpu as pltpu
from jax.sharding import PartitionSpec as P

LY = 32
LZ = 32
MESH = pl.DeviceIdType.MESH
F32 = jnp.float32
BF16 = jnp.bfloat16


def split(value):
    high = value.astype(BF16)
    low = (value - high.astype(F32)).astype(BF16)
    return high, low


def mxu(left, right):
    return lax.dot_general(left, right, (((1,), (0,)), ((), ())), preferred_element_type=F32)


def complex_block(re, im):
    return jnp.concatenate(
        [jnp.concatenate([re, im], axis=1), jnp.concatenate([-im, re], axis=1)], axis=0
    )


def kernel(
    n, nt, chunk,
    mom_hbm, sink_hbm, pick_hbm, time_hbm, vec_hbm, per_hbm,
    h_out, s_out,
    mom_ref, sink_ref, pick_ref, time_ref,
    ab, trans, trig, acc, per, part, rxq, rx1, s1, rx2, full, tabuf, src, half,
    int_sem, vec_sem, per_sem, rs_s, rs_r, ta_s, ta_r, sl_s, sl_r,
    x1_s, x1_r, x2_s, x2_r, x3_s, x3_r,
):
    nmom = part.shape[0]
    rank = part.shape[-1]
    colours, sites = ab.shape[0], ab.shape[1]
    blocks = h_out.shape[1] // rank
    rows = rank // n
    hrows = rank // 2
    g = lax.axis_index("gx")
    t = lax.axis_index("ta")
    core = lax.rem(g, 2)
    partner = g + 1 - 2 * core
    chips = n // 2
    chip = lax.div(g, 2)
    own = lax.rem(core + chip, 2)

    def ahead(d):
        return lax.rem(g + d, n)

    def across(d):
        other = lax.rem(chip + d, chips)
        return 2 * other + lax.rem(own + other, 2)

    def remote(src_ref, dst_ref, ss, rs, **where):
        return pltpu.make_async_remote_copy(
            src_ref=src_ref, dst_ref=dst_ref, send_sem=ss, recv_sem=rs,
            device_id=where, device_id_type=MESH,
        )

    integers = [
        pltpu.make_async_copy(where, to, int_sem.at[i])
        for i, (where, to) in enumerate(
            [(mom_hbm, mom_ref), (sink_hbm, sink_ref), (pick_hbm, pick_ref), (time_hbm, time_ref)]
        )
    ]
    for load in integers:
        load.start()
    barrier = pltpu.get_barrier_semaphore()
    for d in range(1, n):
        pl.semaphore_signal(barrier, inc=1, device_id={"gx": ahead(d)}, device_id_type=MESH)
    for d in range(1, nt):
        pl.semaphore_signal(
            barrier, inc=1, device_id={"ta": lax.rem(t + d, nt)}, device_id_type=MESH
        )

    lead = sites // 2
    pieces = [(0, 0, lead), (0, lead, sites)] + [(col, 0, sites) for col in range(1, colours)]
    loads = []
    for i, (col, lo, hi) in enumerate(pieces):
        for ri in range(2):
            load = pltpu.make_async_copy(
                vec_hbm.at[0, ri, col, lo:hi],
                ab.at[col, lo:hi, ri * rank : (ri + 1) * rank],
                vec_sem.at[i, ri],
            )
            load.start()
            loads.append(load)
    per_load = pltpu.make_async_copy(per_hbm.at[0], per, per_sem)
    per_load.start()

    for load in integers:
        load.wait()

    slab_x = sites // (LY * LZ)
    shape = (8, sites)
    row = lax.broadcasted_iota(jnp.int32, shape, 0)
    site = lax.broadcasted_iota(jnp.int32, shape, 1)

    def component(axis):
        value = jnp.zeros(shape, F32)
        for m in range(nmom):
            value = jnp.where(row == m, mom_ref[m, axis].astype(F32), value)
        return value

    x = (g * slab_x + lax.shift_right_logical(site, int(math.log2(LY * LZ)))).astype(F32)
    y = (lax.shift_right_logical(site, int(math.log2(LZ))) & (LY - 1)).astype(F32)
    z = (site & (LZ - 1)).astype(F32)
    turns = (
        component(0) * x * (1.0 / (slab_x * n))
        + component(1) * y * (1.0 / LY)
        + component(2) * z * (1.0 / LZ)
    )
    turns = turns - jnp.floor(turns + 0.5)
    angle = (2.0 * math.pi) * turns
    trig[0] = jnp.cos(angle)
    trig[1] = jnp.sin(angle)

    scale = 1.0 / math.sqrt(colours * sites * n)

    def accumulate(p, col, lo, hi):
        for i in range(lo, hi, chunk):
            at = slice(i, i + chunk)
            a = trans[col, 0, :, at]
            b = trans[col, 1, :, at]
            c = trig[0, p : p + 1, at]
            s = trig[1, p : p + 1, at]
            for k, phased in enumerate((a * c + b * s, b * c - a * s)):
                product = mxu(phased.astype(BF16), ab[col, at, :])
                if col == 0 and i == 0:
                    acc[k] = product
                else:
                    acc[k] += product

    def finish(p):
        part[p, 0] = (acc[0, :, :rank] + acc[1, :, rank:]).T * scale
        part[p, 1] = (acc[1, :, :rank] - acc[0, :, rank:]).T * scale

    def band(at, size):
        return pl.ds(pl.multiple_of(at * size, size), size)

    sends = []

    def quarter(owner):
        part_of = lax.rem(lax.rem(owner, 2) + lax.div(owner, 2), 2)
        at = part_of * hrows + lax.div(owner, 2) * rows
        return pl.ds(pl.multiple_of(at, rows), rows)

    mine = quarter(g)
    order = sorted(range(1, n), key=lambda d: d % 2)

    def rs_copy(d):
        return remote(
            part.at[0, :, quarter(ahead(d))], rxq.at[d - 1], rs_s.at[d - 1], rs_r.at[d - 1],
            gx=ahead(d),
        )

    def ta_copy(d):
        return remote(
            tabuf.at[t], tabuf.at[t], ta_s.at[d - 1], ta_r.at[d - 1], ta=lax.rem(t + d, nt)
        )

    def sl_copy(d):
        return remote(
            src.at[:, mine], src.at[:, mine], sl_s.at[d - 1], sl_r.at[d - 1], gx=ahead(d)
        )

    def x1_copy(p):
        return remote(
            part.at[p, :, band(1 - own, hrows)], rx1.at[p], x1_s.at[p], x1_r.at[p],
            gx=partner,
        )

    def x2_copy(p, d):
        return remote(
            s1.at[p], rx2.at[p, d - 1], x2_s.at[p, d - 1], x2_r.at[p, d - 1],
            gx=across(d),
        )

    def sink_copy(d):
        rows_out = full.at[0, :, mine]
        return remote(
            rows_out, rows_out, x2_s.at[0, d - 1], x2_r.at[0, d - 1], gx=across(d)
        )

    def x3_copy(p):
        keep = full.at[p, :, band(own, hrows)]
        return remote(keep, keep, x3_s.at[p], x3_r.at[p], gx=partner)

    def go(copy):
        copy.start()
        sends.append(copy)

    def p0_scatter():
        total = part[0, :, mine]
        for d in range(1, n):
            rs_copy(d).wait_recv()
            total = total + rxq[d - 1]
        tabuf[t] = total
        for d in range(1, nt):
            go(ta_copy(d))
        full[0, :, mine] = total
        for d in range(1, chips):
            go(sink_copy(d))

    def p0_select():
        for d in range(1, nt):
            ta_copy(d).wait_recv()
        root = lax.rem(time_ref[0], nt)
        src[:, mine] = tabuf[root]
        for d in order:
            go(sl_copy(d))

    def step2(p):
        x1_copy(p).wait_recv()
        s1[p] = part[p, :, band(own, hrows)] + rx1[p]
        for d in range(1, chips):
            go(x2_copy(p, d))

    def p0_sink():
        for d in range(1, chips):
            sink_copy(d).wait_recv()
        go(x3_copy(0))

    def step3(p):
        total = s1[p]
        for d in range(1, chips):
            x2_copy(p, d).wait_recv()
            total = total + rx2[p, d - 1]
        full[p, :, band(own, hrows)] = total
        go(x3_copy(p))

    for i, (col, lo, hi) in enumerate(pieces):
        loads[2 * i].wait()
        loads[2 * i + 1].wait()
        for ri in range(2):
            trans[col, ri, :, lo:hi] = ab[col, lo:hi, ri * rank : (ri + 1) * rank].T.astype(F32)
        accumulate(0, col, lo, hi)
    finish(0)
    pl.semaphore_wait(barrier, n + nt - 2)
    for d in order:
        go(rs_copy(d))
    for p in range(1, nmom):
        for col in range(colours):
            accumulate(p, col, 0, sites)
            if p > 2 and col == 0:
                step2(p - 2)
        if p == nmom - 1:
            p0_scatter()
            if p > 1:
                step2(p - 1)
        finish(p)
        go(x1_copy(p))
    if nmom > 1:
        step2(nmom - 1)
    else:
        p0_scatter()
    for p in range(1, nmom - 1):
        step3(p)
    p0_sink()
    p0_select()
    if nmom > 1:
        step3(nmom - 1)

    per_load.wait()
    for p in range(nmom):
        x3_copy(p).wait_recv()
    for j in range(blocks):
        sink = sink_ref[g * blocks + j]
        pick = pick_ref[g * blocks + j]
        e_high, e_low = split(jnp.concatenate([full[sink, 0], full[sink, 1]], axis=1))
        spin = complex_block(per[pick, 0], per[pick, 1])
        half[j * rank : (j + 1) * rank] = mxu(e_high, spin) + mxu(e_low, spin)
    h_out[0], h_out[1] = split(half[...] * (1.0 / math.sqrt(rank)))
    for d in range(1, n):
        sl_copy(d).wait_recv()
    s_out[0], s_out[1] = split(complex_block(src[0], src[1]))
    for copy in sends:
        copy.wait_send()


def close(h_ref, s_ref, out_hbm, outbuf, sems):
    blocks = outbuf.shape[0]
    rank = outbuf.shape[-1]
    stores = []
    for j in range(blocks):
        at = slice(j * rank, (j + 1) * rank)
        corr = (
            mxu(h_ref[0, at], s_ref[0]) + mxu(h_ref[0, at], s_ref[1]) + mxu(h_ref[1, at], s_ref[0])
        )
        outbuf[j, 0] = corr[:, :rank]
        outbuf[j, 1] = corr[:, rank:]
        store = pltpu.make_async_copy(outbuf.at[j], out_hbm.at[0, j], sems.at[j])
        store.start()
        stores.append(store)
    for store in stores:
        store.wait()


def in_hbm(array):
    return pltpu.with_memory_space_constraint(array, pltpu.HBM)


def body(vectors, peramb, momenta, sink_mom, spin_pick, src_time):
    n = lax.axis_size("gx")
    nt = lax.axis_size("ta")
    colours, sites, rank = vectors.shape[2:]
    nmom = momenta.shape[0]
    spins = sink_mom.shape[0]
    blocks = spins // n
    rows = rank // n
    chips = n // 2
    chunk = min(1024, sites // 2)
    dma = pltpu.SemaphoreType.DMA
    hbm = pl.BlockSpec(memory_space=pl.ANY)
    h, s = pl.pallas_call(
        functools.partial(kernel, n, nt, chunk),
        out_shape=(
            pltpu.VMEM((2, blocks * rank, 2 * rank), BF16),
            pltpu.VMEM((2, 2 * rank, 2 * rank), BF16),
        ),
        in_specs=[hbm] * 6,
        out_specs=(pl.BlockSpec(memory_space=pltpu.VMEM),) * 2,
        scratch_shapes=[
            pltpu.SMEM(momenta.shape, jnp.int32),
            pltpu.SMEM(sink_mom.shape, jnp.int32),
            pltpu.SMEM(spin_pick.shape, jnp.int32),
            pltpu.SMEM(src_time.shape, jnp.int32),
            pltpu.VMEM((colours, sites, 2 * rank), BF16),
            pltpu.VMEM((colours, 2, rank, sites), F32),
            pltpu.VMEM((2, 8, sites), F32),
            pltpu.VMEM((2, rank, 2 * rank), F32),
            pltpu.VMEM(peramb.shape[1:], BF16),
            pltpu.VMEM((nmom, 2, rank, rank), F32),
            pltpu.VMEM((n - 1, 2, rows, rank), F32),
            pltpu.VMEM((nmom, 2, rank // 2, rank), F32),
            pltpu.VMEM((nmom, 2, rank // 2, rank), F32),
            pltpu.VMEM((nmom, max(chips - 1, 1), 2, rank // 2, rank), F32),
            pltpu.VMEM((nmom, 2, rank, rank), F32),
            pltpu.VMEM((nt, 2, rows, rank), F32),
            pltpu.VMEM((2, rank, rank), F32),
            pltpu.VMEM((blocks * rank, 2 * rank), F32),
            dma((4,)),
            dma((colours + 1, 2)),
            dma,
            dma((n - 1,)), dma((n - 1,)),
            dma((max(nt - 1, 1),)), dma((max(nt - 1, 1),)),
            dma((n - 1,)), dma((n - 1,)),
            dma((nmom,)), dma((nmom,)),
            dma((nmom, max(chips - 1, 1))), dma((nmom, max(chips - 1, 1))),
            dma((nmom,)), dma((nmom,)),
        ],
        compiler_params=pltpu.CompilerParams(
            collective_id=0, has_side_effects=True, vmem_limit_bytes=50*2**20
        ),
    )(
        in_hbm(momenta), in_hbm(sink_mom), in_hbm(spin_pick), src_time,
        in_hbm(vectors), in_hbm(peramb),
    )
    return pl.pallas_call(
        close,
        out_shape=jax.ShapeDtypeStruct((1, blocks, 2, rank, rank), F32),
        in_specs=[pl.BlockSpec(memory_space=pltpu.VMEM)] * 2,
        out_specs=hbm,
        scratch_shapes=[pltpu.VMEM((blocks, 2, rank, rank), F32), dma((blocks,))],
        compiler_params=pltpu.CompilerParams(vmem_limit_bytes=8 * 2**20),
    )(h, s)


def solution(mesh):
    placed = (
        P(("grp", "ta"), None, None, "gx", None),
        P(("grp", "ta"), None, None, None, None),
        P("grp", None),
        P("grp"),
        P("grp"),
        P("grp"),
    )
    return jax.shard_map(
        body,
        mesh=mesh,
        in_specs=placed,
        out_specs=P(("grp", "ta"), "gx", None, None, None),
        check_vma=False,
    )
```

```python
import functools
import math

import jax
import jax.numpy as jnp
from jax import lax
from jax.experimental import pallas as pl
from jax.experimental.pallas import tpu as pltpu
from jax.sharding import PartitionSpec as P

LY = 32
LZ = 32
MESH = pl.DeviceIdType.MESH
F32 = jnp.float32
BF16 = jnp.bfloat16


def split(value):
    high = value.astype(BF16)
    low = (value - high.astype(F32)).astype(BF16)
    return high, low


def mxu(left, right):
    return lax.dot_general(left, right, (((1,), (0,)), ((), ())), preferred_element_type=F32)


def complex_block(re, im):
    return jnp.concatenate(
        [jnp.concatenate([re, im], axis=1), jnp.concatenate([-im, re], axis=1)], axis=0
    )


def kernel(
    n, nt, chunk,
    mom_hbm, sink_hbm, pick_hbm, time_hbm, vec_hbm, per_hbm,
    h_out, s_out,
    mom_ref, sink_ref, pick_ref, time_ref,
    ab, trans, trig, acc, per, part, rxq, rx1, s1, rx2, full, tabuf, src, half,
    int_sem, vec_sem, per_sem, rs_s, rs_r, ta_s, ta_r, sl_s, sl_r,
    x1_s, x1_r, x2_s, x2_r, x3_s, x3_r,
):
    nmom = part.shape[0]
    rank = part.shape[-1]
    colours, sites = ab.shape[0], ab.shape[1]
    blocks = h_out.shape[1] // rank
    rows = rank // n
    hrows = rank // 2
    g = lax.axis_index("gx")
    t = lax.axis_index("ta")
    core = lax.rem(g, 2)
    partner = g + 1 - 2 * core
    chips = n // 2

    def ahead(d):
        return lax.rem(g + d, n)

    def remote(src_ref, dst_ref, ss, rs, **where):
        return pltpu.make_async_remote_copy(
            src_ref=src_ref, dst_ref=dst_ref, send_sem=ss, recv_sem=rs,
            device_id=where, device_id_type=MESH,
        )

    integers = [
        pltpu.make_async_copy(where, to, int_sem.at[i])
        for i, (where, to) in enumerate(
            [(mom_hbm, mom_ref), (sink_hbm, sink_ref), (pick_hbm, pick_ref), (time_hbm, time_ref)]
        )
    ]
    for load in integers:
        load.start()
    barrier = pltpu.get_barrier_semaphore()
    for d in range(1, n):
        pl.semaphore_signal(barrier, inc=1, device_id={"gx": ahead(d)}, device_id_type=MESH)
    for d in range(1, nt):
        pl.semaphore_signal(
            barrier, inc=1, device_id={"ta": lax.rem(t + d, nt)}, device_id_type=MESH
        )

    lead = sites // 2
    pieces = [(0, 0, lead), (0, lead, sites)] + [(col, 0, sites) for col in range(1, colours)]
    loads = []
    for i, (col, lo, hi) in enumerate(pieces):
        for ri in range(2):
            load = pltpu.make_async_copy(
                vec_hbm.at[0, ri, col, lo:hi],
                ab.at[col, lo:hi, ri * rank : (ri + 1) * rank],
                vec_sem.at[i, ri],
            )
            load.start()
            loads.append(load)
    per_load = pltpu.make_async_copy(per_hbm.at[0], per, per_sem)
    per_load.start()

    for load in integers:
        load.wait()

    slab_x = sites // (LY * LZ)
    shape = (8, sites)
    row = lax.broadcasted_iota(jnp.int32, shape, 0)
    site = lax.broadcasted_iota(jnp.int32, shape, 1)

    def component(axis):
        value = jnp.zeros(shape, F32)
        for m in range(nmom):
            value = jnp.where(row == m, mom_ref[m, axis].astype(F32), value)
        return value

    x = (g * slab_x + lax.shift_right_logical(site, int(math.log2(LY * LZ)))).astype(F32)
    y = (lax.shift_right_logical(site, int(math.log2(LZ))) & (LY - 1)).astype(F32)
    z = (site & (LZ - 1)).astype(F32)
    turns = (
        component(0) * x * (1.0 / (slab_x * n))
        + component(1) * y * (1.0 / LY)
        + component(2) * z * (1.0 / LZ)
    )
    turns = turns - jnp.floor(turns + 0.5)
    angle = (2.0 * math.pi) * turns
    trig[0] = jnp.cos(angle)
    trig[1] = jnp.sin(angle)

    scale = 1.0 / math.sqrt(colours * sites * n)

    def accumulate(p, col, lo, hi):
        for i in range(lo, hi, chunk):
            at = slice(i, i + chunk)
            a = trans[col, 0, :, at]
            b = trans[col, 1, :, at]
            c = trig[0, p : p + 1, at]
            s = trig[1, p : p + 1, at]
            for k, phased in enumerate((a * c + b * s, b * c - a * s)):
                product = mxu(phased.astype(BF16), ab[col, at, :])
                if col == 0 and i == 0:
                    acc[k] = product
                else:
                    acc[k] += product

    def finish(p):
        part[p, 0] = (acc[0, :, :rank] + acc[1, :, rank:]).T * scale
        part[p, 1] = (acc[1, :, :rank] - acc[0, :, rank:]).T * scale

    def band(at, size):
        return pl.ds(pl.multiple_of(at * size, size), size)

    sends = []

    def quarter(owner):
        at = lax.rem(owner, 2) * hrows + lax.div(owner, 2) * rows
        return pl.ds(pl.multiple_of(at, rows), rows)

    mine = quarter(g)
    order = sorted(range(1, n), key=lambda d: d % 2)

    def rs_copy(d):
        return remote(
            part.at[0, :, quarter(ahead(d))], rxq.at[d - 1], rs_s.at[d - 1], rs_r.at[d - 1],
            gx=ahead(d),
        )

    def ta_copy(d):
        return remote(
            tabuf.at[t], tabuf.at[t], ta_s.at[d - 1], ta_r.at[d - 1], ta=lax.rem(t + d, nt)
        )

    def sl_copy(d):
        return remote(
            src.at[:, mine], src.at[:, mine], sl_s.at[d - 1], sl_r.at[d - 1], gx=ahead(d)
        )

    def x1_copy(p):
        return remote(
            part.at[p, :, band(1 - core, hrows)], rx1.at[p], x1_s.at[p], x1_r.at[p],
            gx=partner,
        )

    def x2_copy(p, d):
        return remote(
            s1.at[p], rx2.at[p, d - 1], x2_s.at[p, d - 1], x2_r.at[p, d - 1],
            gx=ahead(2 * d),
        )

    def sink_copy(d):
        rows_out = full.at[0, :, mine]
        return remote(
            rows_out, rows_out, x2_s.at[0, d - 1], x2_r.at[0, d - 1], gx=ahead(2 * d)
        )

    def x3_copy(p):
        keep = full.at[p, :, band(core, hrows)]
        return remote(keep, keep, x3_s.at[p], x3_r.at[p], gx=partner)

    def go(copy):
        copy.start()
        sends.append(copy)

    def p0_scatter():
        total = part[0, :, mine]
        for d in range(1, n):
            rs_copy(d).wait_recv()
            total = total + rxq[d - 1]
        tabuf[t] = total
        for d in range(1, nt):
            go(ta_copy(d))
        full[0, :, mine] = total
        for d in range(1, chips):
            go(sink_copy(d))

    def p0_select():
        for d in range(1, nt):
            ta_copy(d).wait_recv()
        root = lax.rem(time_ref[0], nt)
        src[:, mine] = tabuf[root]
        for d in order:
            go(sl_copy(d))

    def step2(p):
        x1_copy(p).wait_recv()
        s1[p] = part[p, :, band(core, hrows)] + rx1[p]
        for d in range(1, chips):
            go(x2_copy(p, d))

    def p0_sink():
        for d in range(1, chips):
            sink_copy(d).wait_recv()
        go(x3_copy(0))

    def step3(p):
        total = s1[p]
        for d in range(1, chips):
            x2_copy(p, d).wait_recv()
            total = total + rx2[p, d - 1]
        full[p, :, band(core, hrows)] = total
        go(x3_copy(p))

    for i, (col, lo, hi) in enumerate(pieces):
        loads[2 * i].wait()
        loads[2 * i + 1].wait()
        for ri in range(2):
            trans[col, ri, :, lo:hi] = ab[col, lo:hi, ri * rank : (ri + 1) * rank].T.astype(F32)
        accumulate(0, col, lo, hi)
    finish(0)
    pl.semaphore_wait(barrier, n + nt - 2)
    for d in order:
        go(rs_copy(d))
    for p in range(1, nmom):
        for col in range(colours):
            accumulate(p, col, 0, sites)
            if p > 2 and col == 0:
                step2(p - 2)
        if p == nmom - 1:
            p0_scatter()
            if p > 1:
                step2(p - 1)
        finish(p)
        go(x1_copy(p))
    if nmom > 1:
        step2(nmom - 1)
    else:
        p0_scatter()
    for p in range(1, nmom - 1):
        step3(p)
    p0_sink()
    p0_select()
    if nmom > 1:
        step3(nmom - 1)

    per_load.wait()
    for p in range(nmom):
        x3_copy(p).wait_recv()
    for j in range(blocks):
        sink = sink_ref[g * blocks + j]
        pick = pick_ref[g * blocks + j]
        e_high, e_low = split(jnp.concatenate([full[sink, 0], full[sink, 1]], axis=1))
        spin = complex_block(per[pick, 0], per[pick, 1])
        half[j * rank : (j + 1) * rank] = mxu(e_high, spin) + mxu(e_low, spin)
    h_out[0], h_out[1] = split(half[...] * (1.0 / math.sqrt(rank)))
    for d in range(1, n):
        sl_copy(d).wait_recv()
    s_out[0], s_out[1] = split(complex_block(src[0], src[1]))
    for copy in sends:
        copy.wait_send()


def close(h_ref, s_ref, out_hbm, outbuf, sems):
    blocks = outbuf.shape[0]
    rank = outbuf.shape[-1]
    stores = []
    for j in range(blocks):
        at = slice(j * rank, (j + 1) * rank)
        corr = (
            mxu(h_ref[0, at], s_ref[0]) + mxu(h_ref[0, at], s_ref[1]) + mxu(h_ref[1, at], s_ref[0])
        )
        outbuf[j, 0] = corr[:, :rank]
        outbuf[j, 1] = corr[:, rank:]
        store = pltpu.make_async_copy(outbuf.at[j], out_hbm.at[0, j], sems.at[j])
        store.start()
        stores.append(store)
    for store in stores:
        store.wait()


def in_hbm(array):
    return pltpu.with_memory_space_constraint(array, pltpu.HBM)


def body(vectors, peramb, momenta, sink_mom, spin_pick, src_time):
    n = lax.axis_size("gx")
    nt = lax.axis_size("ta")
    colours, sites, rank = vectors.shape[2:]
    nmom = momenta.shape[0]
    spins = sink_mom.shape[0]
    blocks = spins // n
    rows = rank // n
    chips = n // 2
    chunk = min(1024, sites // 2)
    dma = pltpu.SemaphoreType.DMA
    hbm = pl.BlockSpec(memory_space=pl.ANY)
    h, s = pl.pallas_call(
        functools.partial(kernel, n, nt, chunk),
        out_shape=(
            pltpu.VMEM((2, blocks * rank, 2 * rank), BF16),
            pltpu.VMEM((2, 2 * rank, 2 * rank), BF16),
        ),
        in_specs=[hbm] * 6,
        out_specs=(pl.BlockSpec(memory_space=pltpu.VMEM),) * 2,
        scratch_shapes=[
            pltpu.SMEM(momenta.shape, jnp.int32),
            pltpu.SMEM(sink_mom.shape, jnp.int32),
            pltpu.SMEM(spin_pick.shape, jnp.int32),
            pltpu.SMEM(src_time.shape, jnp.int32),
            pltpu.VMEM((colours, sites, 2 * rank), BF16),
            pltpu.VMEM((colours, 2, rank, sites), F32),
            pltpu.VMEM((2, 8, sites), F32),
            pltpu.VMEM((2, rank, 2 * rank), F32),
            pltpu.VMEM(peramb.shape[1:], BF16),
            pltpu.VMEM((nmom, 2, rank, rank), F32),
            pltpu.VMEM((n - 1, 2, rows, rank), F32),
            pltpu.VMEM((nmom, 2, rank // 2, rank), F32),
            pltpu.VMEM((nmom, 2, rank // 2, rank), F32),
            pltpu.VMEM((nmom, max(chips - 1, 1), 2, rank // 2, rank), F32),
            pltpu.VMEM((nmom, 2, rank, rank), F32),
            pltpu.VMEM((nt, 2, rows, rank), F32),
            pltpu.VMEM((2, rank, rank), F32),
            pltpu.VMEM((blocks * rank, 2 * rank), F32),
            dma((4,)),
            dma((colours + 1, 2)),
            dma,
            dma((n - 1,)), dma((n - 1,)),
            dma((max(nt - 1, 1),)), dma((max(nt - 1, 1),)),
            dma((n - 1,)), dma((n - 1,)),
            dma((nmom,)), dma((nmom,)),
            dma((nmom, max(chips - 1, 1))), dma((nmom, max(chips - 1, 1))),
            dma((nmom,)), dma((nmom,)),
        ],
        compiler_params=pltpu.CompilerParams(
            collective_id=0, has_side_effects=True, vmem_limit_bytes=50*2**20
        ),
    )(
        in_hbm(momenta), in_hbm(sink_mom), in_hbm(spin_pick), src_time,
        in_hbm(vectors), in_hbm(peramb),
    )
    return pl.pallas_call(
        close,
        out_shape=jax.ShapeDtypeStruct((1, blocks, 2, rank, rank), F32),
        in_specs=[pl.BlockSpec(memory_space=pltpu.VMEM)] * 2,
        out_specs=hbm,
        scratch_shapes=[pltpu.VMEM((blocks, 2, rank, rank), F32), dma((blocks,))],
        compiler_params=pltpu.CompilerParams(vmem_limit_bytes=8 * 2**20),
    )(h, s)


def solution(mesh):
    placed = (
        P(("grp", "ta"), None, None, "gx", None),
        P(("grp", "ta"), None, None, None, None),
        P("grp", None),
        P("grp"),
        P("grp"),
        P("grp"),
    )
    return jax.shard_map(
        body,
        mesh=mesh,
        in_specs=placed,
        out_specs=P(("grp", "ta"), "gx", None, None, None),
        check_vma=False,
    )
```
